32 devices in a mesh: member: 4 (over y, x), lat: 8 (over z, core).
Axes of the slice: x: 2, y: 2, z: 4, core: 2. Of those that a mesh axis runs over, the one named last changes fastest.
Arguments:
- initial_states: float32 [4, 16, 80, 128], P('member', 'lat'), may hold values from -6 to 6
- targets: float32 [2, 16, 80, 128], P(None, 'lat'), may hold values from -6 to 6
- lat_weight: float32 [16], P('lat'), may hold values from 0.3 to 3
- weight_in: float32 [256, 720], replicated, may hold values from -0.21875 to 0.21875
- weight_out: float32 [80, 2304], replicated, may hold values from -0.125 to 0.125
- hidden_bias: float32 [256], replicated, may hold values from -4 to 4
Outputs:
- state_grad: float32 [4, 16, 80, 128], P('member', 'lat')
- loss: float32 [], replicated
The draws below stay inside these ranges and needn't reach their ends.
All inputs are finite; a program needn't handle non-finite values.
Results may differ from the reference program's by a relative error of at most 0.00023.
Values sent between devices are 32-bit elements; how exact they have to be, the bound alone decides.
A program may use at most 64 MiB of HBM per device.

```python
import math
import jax
import jax.numpy as jnp
from jax import lax

VARS = 80
CH = 256
LON = 128
STEPS = 2
MEMBERS = 4
NLAT = 16


def shard_levels(stream_key, extent, pieces, low, high):
    level, own = 1.0, jax.random.fold_in(stream_key, 6)
    for axis_at, parts in pieces:
        steps = jnp.exp(jax.random.uniform(jax.random.fold_in(own, axis_at), (parts,), jnp.float32, low / len(pieces), high / len(pieces)))
        level = level * jnp.repeat(steps, extent[axis_at] // parts).reshape([-1 if axis == axis_at else 1 for axis in range(len(extent))])
    return level


def gaussian(stream_key, extent, width, bound, split=(), kind=jnp.bfloat16):
    loudness = shard_levels(stream_key, extent, split, -0.22, 0.18) if split else 1.0
    array = jax.random.normal(stream_key, extent, jnp.float32) * width * loudness
    return jnp.minimum(jnp.maximum(array, -bound), bound).astype(kind)


def setup_inputs(seed: int = 0) -> dict:
    key_of = jax.random.split(jax.random.key(seed), 7)
    initial_states = gaussian(key_of[0], (MEMBERS, NLAT, VARS, LON), 1.0, 6.0, ((0, 4), (1, 8)), jnp.float32)
    targets = gaussian(key_of[1], (STEPS, NLAT, VARS, LON), 1.0, 6.0, ((1, 8),), jnp.float32)
    lat_weight = jnp.clip(jnp.exp(math.log(3.0) - 2.3025851 * jax.random.uniform(key_of[2], (NLAT,), jnp.float32) ** shard_levels(key_of[2], (NLAT,), ((0, 8),), -0.2, 0.2)), 0.3, 3.0)
    weight_in = gaussian(key_of[3], (CH, 9 * VARS), (9 * VARS) ** -0.5, 0.21875, (), jnp.float32)
    weight_out = gaussian(key_of[4], (VARS, 9 * CH), (9 * CH) ** -0.5, 0.125, (), jnp.float32)
    hidden_bias = gaussian(key_of[5], (CH,), 1.0, 4.0, (), jnp.float32)
    return dict(initial_states=initial_states, targets=targets, lat_weight=lat_weight, weight_in=weight_in, weight_out=weight_out, hidden_bias=hidden_bias)


smooth_width = 0.1

def smooth(spread):
    return jnp.sqrt(spread * spread + smooth_width * smooth_width)

def convolve(field, matrix):
    height, channels, columns = field.shape
    padded = jnp.pad(field, ((1, 1), (0, 0), (1, 1)))
    blocks = matrix.reshape(matrix.shape[0], 9, channels)
    result = jnp.zeros((height, matrix.shape[0], columns), jnp.float32)
    for across in range(3):
        for along in range(3):
            result = result + jnp.einsum('oc,rcl->rol', blocks[:, 3 * across + along], padded[across:across + height, :, along:along + columns], precision=lax.Precision.HIGHEST)
    return result

def summed_loss(initial_states, targets, lat_weight, weight_in, weight_out, hidden_bias):

    def advance(member_field):
        before = convolve(member_field, weight_in) + hidden_bias[None, :, None]
        return member_field + convolve(jax.nn.gelu(before), weight_out)
    field = initial_states
    result = jnp.zeros((), jnp.float32)
    weights = lat_weight[:, None, None]
    for rollout in range(STEPS):
        field = lax.map(advance, field)
        direct = lax.optimization_barrier(jnp.sum(smooth(field - targets[rollout][None]), axis=0))

        def pair_row(single, field=field):
            return lax.optimization_barrier(jnp.sum(smooth(single[None] - field), axis=0))
        pairs = lax.optimization_barrier(jnp.sum(lax.map(pair_row, field), axis=0))
        result = result + jnp.sum(weights * (direct - pairs / (2.0 * (MEMBERS - 1))))
    return result

def reference(initial_states, targets, lat_weight, weight_in, weight_out, hidden_bias):
    result, gradient = jax.value_and_grad(summed_loss)(initial_states, targets, lat_weight, weight_in, weight_out, hidden_bias)
    loss = result / (MEMBERS * STEPS * NLAT * VARS * LON)
    return (gradient, loss)
```

```python
import functools

import jax
import jax.numpy as jnp
from jax import lax
from jax.experimental import pallas as pl
from jax.experimental.pallas import tpu as pltpu
from jax.sharding import PartitionSpec as P

smooth_width = 0.1
gelu_scale = 0.7978845608028654
gelu_cubic = 0.044715
MESH = pl.DeviceIdType.MESH
F32 = jnp.float32
BF16 = jnp.bfloat16


def split(value):
    high = value.astype(BF16)
    low = (value - high.astype(F32)).astype(BF16)
    return high, low


def shifted(value, tap):
    if tap == 1:
        return value
    columns = value.shape[-1]
    lane = lax.broadcasted_iota(jnp.int32, value.shape, 1)
    if tap == 0:
        return jnp.where(lane == 0, 0.0, pltpu.roll(value, 1, 1))
    return jnp.where(lane == columns - 1, 0.0, pltpu.roll(value, columns - 1, 1))


def dot(left, right):
    return jnp.dot(left, right, preferred_element_type=F32)


def kernel(
    members, bands,
    x_ref, target_ref, lat_ref, w_in_ref, w_out_ref, bias_ref,
    grad_ref, loss_ref,
    halo, others, parts_m, parts_l, fields, grads, part_src,
    win, winb, wout, woutb, tall, wide, s_high, s_low, h_high, h_low, before, slope, loss_grad, bias,
    halo_send, halo_recv, other_send, other_recv, pm_send, pm_recv, pl_send, pl_recv,
):
    steps, rows, chans, cols = target_ref.shape
    hidden = w_in_ref.shape[0]
    taps = 3 * chans
    depth = win.shape[1]
    deep = 3 * hidden
    me_m = lax.axis_index("member")
    me_l = lax.axis_index("lat")
    has_up = me_l > 0
    has_down = me_l < bands - 1

    barrier = pltpu.get_barrier_semaphore()
    for k in range(1, members):
        pl.semaphore_signal(barrier, inc=1, device_id={"member": lax.rem(me_m + k, members)}, device_id_type=MESH)
    for k in range(1, bands):
        pl.semaphore_signal(barrier, inc=1, device_id={"lat": lax.rem(me_l + k, bands)}, device_id_type=MESH)

    @pl.when(jnp.logical_not(has_up))
    def _():
        for n in range(2 * steps):
            halo[n, 0] = jnp.zeros(halo.shape[2:], F32)

    @pl.when(jnp.logical_not(has_down))
    def _():
        for n in range(2 * steps):
            halo[n, 1] = jnp.zeros(halo.shape[2:], F32)

    def to_up(n, source):
        return pltpu.make_async_remote_copy(
            src_ref=source.at[0:2], dst_ref=halo.at[n, 1],
            send_sem=halo_send.at[n, 0], recv_sem=halo_recv.at[n, 1],
            device_id={"lat": jnp.maximum(me_l - 1, 0)}, device_id_type=MESH)

    def to_down(n, source):
        return pltpu.make_async_remote_copy(
            src_ref=source.at[rows - 2:rows], dst_ref=halo.at[n, 0],
            send_sem=halo_send.at[n, 1], recv_sem=halo_recv.at[n, 0],
            device_id={"lat": jnp.minimum(me_l + 1, bands - 1)}, device_id_type=MESH)

    def halo_start(n, source):
        @pl.when(has_up)
        def _():
            to_up(n, source).start()

        @pl.when(has_down)
        def _():
            to_down(n, source).start()

    def halo_wait(n, source):
        @pl.when(has_up)
        def _():
            to_up(n, source).wait_send()
            to_down(n, source).wait_recv()

        @pl.when(has_down)
        def _():
            to_down(n, source).wait_send()
            to_up(n, source).wait_recv()

    def to_member(step, k):
        return pltpu.make_async_remote_copy(
            src_ref=fields.at[step], dst_ref=others.at[step, k - 1],
            send_sem=other_send.at[step, k - 1], recv_sem=other_recv.at[step, k - 1],
            device_id={"member": lax.rem(me_m + k, members)}, device_id_type=MESH)

    pl.semaphore_wait(barrier, members + bands - 2)
    halo_start(0, x_ref)

    wide[:, depth - 128:depth] = jnp.zeros((hidden, 128), F32)
    wide[:, 0:3 * taps] = w_in_ref[...]
    high, low = split(wide[...])
    win[0:hidden] = high
    win[hidden:2 * hidden] = low
    for a in range(3):
        for b in range(3):
            at = (3 * a + b) * hidden
            high, low = split(w_out_ref[:, at:at + hidden])
            wout[b * chans:(b + 1) * chans, a * hidden:(a + 1) * hidden] = high
            wout[taps + b * chans:taps + (b + 1) * chans, a * hidden:(a + 1) * hidden] = low
    bias[...] = jnp.broadcast_to(bias_ref[...], (cols, hidden)).T
    tail = depth * 1 - 3 * taps
    s_high[(rows + 4) * taps:, :] = jnp.zeros((tail, cols), BF16)
    s_low[(rows + 4) * taps:, :] = jnp.zeros((tail, cols), BF16)

    def back_weights():
        tall[...] = wide[...].T
        for a in range(3):
            for b in range(3):
                at = (3 * (2 - a) + 2 - b) * chans
                high, low = split(tall[at:at + chans, :])
                winb[b * chans:(b + 1) * chans, a * hidden:(a + 1) * hidden] = high
                winb[taps + b * chans:taps + (b + 1) * chans, a * hidden:(a + 1) * hidden] = low
        for k in range(9):
            at = (8 - k) * hidden
            tall[k * chans:(k + 1) * chans, :] = w_out_ref[:, at:at + hidden]
        high, low = split(tall[...].T)
        woutb[0:hidden] = high
        woutb[hidden:2 * hidden] = low

    def widen(weights, own, n):
        for j in range(rows + 4):
            if j < 2:
                line = halo[n, 0, j]
            elif j < rows + 2:
                line = own[j - 2]
            else:
                line = halo[n, 1, j - rows - 2]
            for b in range(3):
                high, low = split(shifted(line, b))
                at = j * taps + b * chans
                s_high[at:at + chans, :] = high
                s_low[at:at + chans, :] = low
        right = jnp.concatenate([s_high[j * taps:j * taps + depth, :] for j in range(rows + 2)], axis=1)
        both = dot(weights[...], right)
        right = jnp.concatenate([s_low[j * taps:j * taps + depth, :] for j in range(rows + 2)], axis=1)
        return both[0:hidden] + both[hidden:2 * hidden] + dot(weights[0:hidden, :], right)

    def narrow(weights):
        right = jnp.concatenate([h_high[r * hidden:r * hidden + deep, :] for r in range(rows)], axis=1)
        both = dot(weights[...], right)
        right = jnp.concatenate([h_low[r * hidden:r * hidden + deep, :] for r in range(rows)], axis=1)
        total = both[0:taps] + both[taps:2 * taps] + dot(weights[0:taps, :], right)
        result = []
        for r in range(rows):
            line = total[:, r * cols:(r + 1) * cols]
            result.append(sum(shifted(line[b * chans:(b + 1) * chans], b) for b in range(3)))
        return result

    def put_hidden(j, value):
        if j == 0:
            value = jnp.where(has_up, value, 0.0)
        if j == rows + 1:
            value = jnp.where(has_down, value, 0.0)
        high, low = split(value)
        h_high[j * hidden:(j + 1) * hidden, :] = high
        h_low[j * hidden:(j + 1) * hidden, :] = low

    def fold(value):
        return sum(value[8 * i:8 * i + 8] for i in range(chans // 8))

    def loss_terms(step):
        partial = jnp.zeros((8, cols), F32)
        for r in range(rows):
            weight = lat_ref[0, r]
            mine = fields[step, r]
            error = mine - target_ref[step, r]
            square = error * error + smooth_width * smooth_width
            inverse = lax.rsqrt(square)
            direct = square * inverse
            gradient = error * inverse
            summed = jnp.full(mine.shape, smooth_width, F32)
            slopes = jnp.zeros_like(mine)
            for k in range(1, members):
                spread = mine - others[step, k - 1, r]
                square = spread * spread + smooth_width * smooth_width
                inverse = lax.rsqrt(square)
                summed = summed + square * inverse
                slopes = slopes + spread * inverse
            partial = partial + weight * fold(direct - summed / (2.0 * (members - 1)))
            loss_grad[step, r] = weight * (gradient - slopes / (members - 1))
        return partial

    for step in range(steps):
        own = x_ref if step == 0 else fields.at[step - 1]
        halo_wait(step, own)
        before[...] = widen(win, own, step)
        for j in range(rows + 2):
            value = before[:, j * cols:(j + 1) * cols] + bias[...]
            inner = jnp.tanh(gelu_scale * (value + gelu_cubic * value * value * value))
            put_hidden(j, 0.5 * value * (1.0 + inner))
            slope[step, :, j * cols:(j + 1) * cols] = 0.5 * (1.0 + inner) + 0.5 * value * (1.0 - inner * inner) * (
                gelu_scale * (1.0 + 3.0 * gelu_cubic * value * value))
        change = narrow(wout)
        for r in range(rows):
            fields[step, r] = own[r] + change[r]
        if step < steps - 1:
            halo_start(step + 1, fields.at[step])
        for k in range(1, members):
            to_member(step, k).start()
        if step == 0:
            back_weights()

    partial = jnp.zeros((8, cols), F32)
    for step in range(steps):
        for k in range(1, members):
            to_member(step, k).wait()
        partial = partial + loss_terms(step)

    def part_to_member(k):
        return pltpu.make_async_remote_copy(
            src_ref=part_src.at[0], dst_ref=parts_m.at[me_m],
            send_sem=pm_send.at[k - 1], recv_sem=pm_recv.at[me_m],
            device_id={"member": lax.rem(me_m + k, members)}, device_id_type=MESH)

    def part_from_member(k):
        source = lax.rem(me_m + k, members)
        return pltpu.make_async_remote_copy(
            src_ref=part_src.at[0], dst_ref=parts_m.at[source],
            send_sem=pm_send.at[k - 1], recv_sem=pm_recv.at[source],
            device_id={"member": source}, device_id_type=MESH)

    def part_to_band(k):
        return pltpu.make_async_remote_copy(
            src_ref=part_src.at[1], dst_ref=parts_l.at[me_l],
            send_sem=pl_send.at[k - 1], recv_sem=pl_recv.at[me_l],
            device_id={"lat": lax.rem(me_l + k, bands)}, device_id_type=MESH)

    def part_from_band(k):
        source = lax.rem(me_l + k, bands)
        return pltpu.make_async_remote_copy(
            src_ref=part_src.at[1], dst_ref=parts_l.at[source],
            send_sem=pl_send.at[k - 1], recv_sem=pl_recv.at[source],
            device_id={"lat": source}, device_id_type=MESH)

    part_src[0] = partial

    for step in range(steps - 1, -1, -1):
        n = 2 * steps - 1 - step
        own = grads.at[step]
        for r in range(rows):
            if step == steps - 1:
                grads[step, r] = loss_grad[step, r]
            else:
                grads[step, r] = grads[step + 1, r] + change[r] + loss_grad[step, r]
        halo_start(n, own)
        if step == steps - 1:
            for k in range(1, members):
                part_to_member(k).start()
            parts_m[me_m] = partial
        else:
            if step == steps - 2:
                for k in range(1, members):
                    part_to_member(k).wait_send()
                    part_from_member(k).wait_recv()
                total = sum(parts_m[k] for k in range(members))
                part_src[1] = total
                for k in range(1, bands):
                    part_to_band(k).start()
                parts_l[me_l] = total
        halo_wait(n, own)
        before[...] = widen(woutb, own, n)
        for j in range(rows + 2):
            put_hidden(j, before[:, j * cols:(j + 1) * cols] * slope[step, :, j * cols:(j + 1) * cols])
        change = narrow(winb)

    for r in range(rows):
        grad_ref[r] = grads[0, r] + change[r]
    for k in range(1, bands):
        part_to_band(k).wait_send()
        part_from_band(k).wait_recv()
    total = sum(parts_l[k] for k in range(bands))
    count = members * steps * rows * bands * chans * cols
    loss_ref[0, 0] = jnp.sum(total) / count


def on_device(members, bands, initial_states, targets, lat_weight, weight_in, weight_out, hidden_bias):
    steps, rows, chans, cols = targets.shape
    hidden = weight_in.shape[0]
    taps = 3 * chans
    depth = -(-3 * taps // 256) * 256
    deep = 3 * hidden
    vmem = pl.BlockSpec(memory_space=pltpu.VMEM)
    smem = pl.BlockSpec(memory_space=pltpu.SMEM)
    dma = pltpu.SemaphoreType.DMA
    gradient, loss = pl.pallas_call(
        functools.partial(kernel, members, bands),
        out_shape=(jax.ShapeDtypeStruct((rows, chans, cols), F32), jax.ShapeDtypeStruct((1, 1), F32)),
        in_specs=[vmem, vmem, smem, vmem, vmem, vmem],
        out_specs=(vmem, smem),
        scratch_shapes=[
            pltpu.VMEM((2 * steps, 2, 2, chans, cols), F32),
            pltpu.VMEM((steps, members - 1, rows, chans, cols), F32),
            pltpu.VMEM((members, 8, cols), F32),
            pltpu.VMEM((bands, 8, cols), F32),
            pltpu.VMEM((steps, rows, chans, cols), F32),
            pltpu.VMEM((steps, rows, chans, cols), F32),
            pltpu.VMEM((2, 8, cols), F32),
            pltpu.VMEM((2 * hidden, depth), BF16),
            pltpu.VMEM((2 * taps, deep), BF16),
            pltpu.VMEM((2 * taps, deep), BF16),
            pltpu.VMEM((2 * hidden, depth), BF16),
            pltpu.VMEM((depth, hidden), F32),
            pltpu.VMEM((hidden, depth), F32),
            pltpu.VMEM(((rows + 4) * taps + depth - 3 * taps, cols), BF16),
            pltpu.VMEM(((rows + 4) * taps + depth - 3 * taps, cols), BF16),
            pltpu.VMEM(((rows + 2) * hidden, cols), BF16),
            pltpu.VMEM(((rows + 2) * hidden, cols), BF16),
            pltpu.VMEM((hidden, (rows + 2) * cols), F32),
            pltpu.VMEM((steps, hidden, (rows + 2) * cols), F32),
            pltpu.VMEM((steps, rows, chans, cols), F32),
            pltpu.VMEM((hidden, cols), F32),
            dma((2 * steps, 2)), dma((2 * steps, 2)),
            dma((steps, members - 1)), dma((steps, members - 1)),
            dma((members - 1,)), dma((members,)),
            dma((bands - 1,)), dma((bands,)),
        ],
        compiler_params=pltpu.CompilerParams(collective_id=0, has_side_effects=True),
    )(
        initial_states.reshape(rows, chans, cols), targets, lat_weight.reshape(1, rows),
        weight_in, weight_out, hidden_bias.reshape(1, hidden),
    )
    return gradient.reshape(initial_states.shape), loss.reshape(())


def solution(mesh):
    placed = (P("member", "lat", None, None), P(None, "lat", None, None), P("lat"), P(), P(), P())
    return jax.shard_map(
        functools.partial(on_device, mesh.shape["member"], mesh.shape["lat"]),
        mesh=mesh,
        in_specs=placed,
        out_specs=(P("member", "lat", None, None), P()),
        check_vma=False,
    )
```

```python
import functools

import jax
import jax.numpy as jnp
from jax import lax
from jax.experimental import pallas as pl
from jax.experimental.pallas import tpu as pltpu
from jax.sharding import PartitionSpec as P

smooth_width = 0.1
gelu_scale = 0.7978845608028654
gelu_cubic = 0.044715
MESH = pl.DeviceIdType.MESH
F32 = jnp.float32
BF16 = jnp.bfloat16


def split(value):
    high = value.astype(BF16)
    low = (value - high.astype(F32)).astype(BF16)
    return high, low


def shifted(value, tap):
    if tap == 1:
        return value
    columns = value.shape[-1]
    lane = lax.broadcasted_iota(jnp.int32, value.shape, 1)
    if tap == 0:
        return jnp.where(lane == 0, 0.0, pltpu.roll(value, 1, 1))
    return jnp.where(lane == columns - 1, 0.0, pltpu.roll(value, columns - 1, 1))


def dot(left, right):
    return jnp.dot(left, right, preferred_element_type=F32)


def kernel(
    members, bands,
    x_hbm, target_hbm, lat_hbm, w_in_hbm, w_out_hbm, bias_hbm,
    grad_ref, loss_ref,
    x_ref, target_ref, lat_ref, w_in_ref, w_out_ref, bias_ref, fetch_sem,
    halo, others, parts_m, parts_l, fields, grads, part_src,
    win, winb, wout, woutb, tall, s_high, s_low, h_high, h_low, before, slope, loss_grad, bias,
    halo_send, halo_recv, other_send, other_recv, pm_send, pm_recv, pl_send, pl_recv,
):
    steps, rows, chans, cols = target_ref.shape
    hidden = w_in_ref.shape[1]
    taps = 3 * chans
    depth = win.shape[2]
    deep = 3 * hidden
    me_m = lax.axis_index("member")
    me_l = lax.axis_index("lat")
    has_up = me_l > 0
    has_down = me_l < bands - 1

    fetches = [
        pltpu.make_async_copy(source, target, fetch_sem.at[n])
        for n, (source, target) in enumerate([
            (x_hbm, x_ref), (w_in_hbm, w_in_ref), (w_out_hbm, w_out_ref),
            (bias_hbm, bias_ref), (target_hbm, target_ref), (lat_hbm, lat_ref)])
    ]
    barrier = pltpu.get_barrier_semaphore()
    for k in range(1, members):
        pl.semaphore_signal(barrier, inc=1, device_id={"member": lax.rem(me_m + k, members)}, device_id_type=MESH)
    for k in range(1, bands):
        pl.semaphore_signal(barrier, inc=1, device_id={"lat": lax.rem(me_l + k, bands)}, device_id_type=MESH)

    for fetch in fetches:
        fetch.start()

    @pl.when(jnp.logical_not(has_up))
    def _():
        for n in range(2 * steps):
            halo[n, 0] = jnp.zeros(halo.shape[2:], F32)

    @pl.when(jnp.logical_not(has_down))
    def _():
        for n in range(2 * steps):
            halo[n, 1] = jnp.zeros(halo.shape[2:], F32)

    def to_up(n, source):
        return pltpu.make_async_remote_copy(
            src_ref=source.at[0:2], dst_ref=halo.at[n, 1],
            send_sem=halo_send.at[n, 0], recv_sem=halo_recv.at[n, 1],
            device_id={"lat": jnp.maximum(me_l - 1, 0)}, device_id_type=MESH)

    def to_down(n, source):
        return pltpu.make_async_remote_copy(
            src_ref=source.at[rows - 2:rows], dst_ref=halo.at[n, 0],
            send_sem=halo_send.at[n, 1], recv_sem=halo_recv.at[n, 0],
            device_id={"lat": jnp.minimum(me_l + 1, bands - 1)}, device_id_type=MESH)

    def halo_start(n, source):
        @pl.when(has_up)
        def _():
            to_up(n, source).start()

        @pl.when(has_down)
        def _():
            to_down(n, source).start()

    def halo_wait(n, source):
        @pl.when(has_up)
        def _():
            to_up(n, source).wait_send()
            to_down(n, source).wait_recv()

        @pl.when(has_down)
        def _():
            to_down(n, source).wait_send()
            to_up(n, source).wait_recv()

    def to_member(step, k):
        return pltpu.make_async_remote_copy(
            src_ref=fields.at[step], dst_ref=others.at[step, k - 1],
            send_sem=other_send.at[step, k - 1], recv_sem=other_recv.at[step, k - 1],
            device_id={"member": lax.rem(me_m + k, members)}, device_id_type=MESH)

    fetches[0].wait()
    pl.semaphore_wait(barrier, members + bands - 2)
    halo_start(0, x_ref)

    def put_wide(target, a, block):
        tall[0:taps, :] = block
        high, low = split(tall[...].T)
        target[a, 0:hidden] = high
        target[a, hidden:2 * hidden] = low

    def front_weights():
        for fetch in fetches[1:]:
            fetch.wait()
        tall[taps:, :] = jnp.zeros((depth - taps, hidden), F32)
        for a in range(3):
            put_wide(win, a, w_in_ref[a * taps:(a + 1) * taps, :])
        bias[...] = jnp.broadcast_to(bias_ref[...], (cols, hidden)).T
        for j in range(rows + 4):
            s_high[j * depth + taps:(j + 1) * depth, :] = jnp.zeros((depth - taps, cols), BF16)
            s_low[j * depth + taps:(j + 1) * depth, :] = jnp.zeros((depth - taps, cols), BF16)

    def narrow_weights():
        for a in range(3):
            for b in range(3):
                at = (3 * a + b) * hidden
                high, low = split(w_out_ref[:, at:at + hidden])
                wout[b * chans:(b + 1) * chans, a * hidden:(a + 1) * hidden] = high
                wout[taps + b * chans:taps + (b + 1) * chans, a * hidden:(a + 1) * hidden] = low

    def back_weights():
        for a in range(3):
            for b in range(3):
                at = (3 * (2 - a) + 2 - b) * chans
                high, low = split(w_in_ref[at:at + chans, :])
                winb[b * chans:(b + 1) * chans, a * hidden:(a + 1) * hidden] = high
                winb[taps + b * chans:taps + (b + 1) * chans, a * hidden:(a + 1) * hidden] = low
        for a in range(3):
            at = 3 * (2 - a) * hidden
            put_wide(woutb, a, jnp.concatenate(
                [w_out_ref[:, at + (2 - b) * hidden:at + (3 - b) * hidden] for b in range(3)], axis=0))

    def put_line(i, line):
        for b in range(3):
            high, low = split(shifted(line, b))
            at = i * depth + b * chans
            s_high[at:at + chans, :] = high
            s_low[at:at + chans, :] = low

    def widen_part(weights, inside):
        sums = {}
        for a in range(3):
            lines = [j for j in range(rows + 2) if (2 <= j + a < rows + 2) == inside]
            high = jnp.concatenate([s_high[(j + a) * depth:(j + a + 1) * depth, :] for j in lines], axis=1)
            low = jnp.concatenate([s_low[(j + a) * depth:(j + a + 1) * depth, :] for j in lines], axis=1)
            both = dot(weights[a], high)
            total = both[0:hidden] + both[hidden:2 * hidden] + dot(weights[a, 0:hidden, :], low)
            for n, j in enumerate(lines):
                line = total[:, n * cols:(n + 1) * cols]
                sums[j] = line if j not in sums else sums[j] + line
        return sums

    def widen_own(weights, own):
        for r in range(rows):
            put_line(r + 2, own[r])
        for j, line in widen_part(weights, True).items():
            before[:, j * cols:(j + 1) * cols] = line

    def widen_rest(weights, n):
        for j in range(2):
            put_line(j, halo[n, 0, j])
            put_line(rows + 2 + j, halo[n, 1, j])
        for j, line in widen_part(weights, False).items():
            before[:, j * cols:(j + 1) * cols] += line

    def narrow(weights):
        right = jnp.concatenate([h_high[r * hidden:r * hidden + deep, :] for r in range(rows)], axis=1)
        both = dot(weights[...], right)
        right = jnp.concatenate([h_low[r * hidden:r * hidden + deep, :] for r in range(rows)], axis=1)
        total = both[0:taps] + both[taps:2 * taps] + dot(weights[0:taps, :], right)
        result = []
        for r in range(rows):
            line = total[:, r * cols:(r + 1) * cols]
            result.append(sum(shifted(line[b * chans:(b + 1) * chans], b) for b in range(3)))
        return result

    def put_hidden(j, value):
        if j == 0:
            value = jnp.where(has_up, value, 0.0)
        if j == rows + 1:
            value = jnp.where(has_down, value, 0.0)
        high, low = split(value)
        h_high[j * hidden:(j + 1) * hidden, :] = high
        h_low[j * hidden:(j + 1) * hidden, :] = low

    def fold(value):
        return sum(value[8 * i:8 * i + 8] for i in range(chans // 8))

    def loss_terms(step):
        partial = jnp.zeros((8, cols), F32)
        for r in range(rows):
            weight = lat_ref[0:1, r:r + 1]
            mine = fields[step, r]
            error = mine - target_ref[step, r]
            square = error * error + smooth_width * smooth_width
            inverse = lax.rsqrt(square)
            direct = square * inverse
            gradient = error * inverse
            summed = jnp.full(mine.shape, smooth_width, F32)
            slopes = jnp.zeros_like(mine)
            for k in range(1, members):
                spread = mine - others[step, k - 1, r]
                square = spread * spread + smooth_width * smooth_width
                inverse = lax.rsqrt(square)
                summed = summed + square * inverse
                slopes = slopes + spread * inverse
            partial = partial + weight * fold(direct - summed / (2.0 * (members - 1)))
            loss_grad[step, r] = weight * (gradient - slopes / (members - 1))
        return partial

    for step in range(steps):
        own = x_ref if step == 0 else fields.at[step - 1]
        if step == 0:
            front_weights()
        widen_own(win, own)
        if step == 0:
            narrow_weights()
        halo_wait(step, own)
        widen_rest(win, step)
        for j in range(rows + 2):
            value = before[:, j * cols:(j + 1) * cols] + bias[...]
            inner = jnp.tanh(gelu_scale * (value + gelu_cubic * value * value * value))
            put_hidden(j, 0.5 * value * (1.0 + inner))
            slope[step, :, j * cols:(j + 1) * cols] = 0.5 * (1.0 + inner) + 0.5 * value * (1.0 - inner * inner) * (
                gelu_scale * (1.0 + 3.0 * gelu_cubic * value * value))
        change = narrow(wout)
        for r in range(rows):
            fields[step, r] = own[r] + change[r]
        if step < steps - 1:
            halo_start(step + 1, fields.at[step])
        for k in range(1, members):
            to_member(step, k).start()
        if step == 0:
            back_weights()

    partial = jnp.zeros((8, cols), F32)
    for step in range(steps):
        for k in range(1, members):
            to_member(step, k).wait()
        partial = partial + loss_terms(step)

    def part_to_member(k):
        return pltpu.make_async_remote_copy(
            src_ref=part_src.at[0], dst_ref=parts_m.at[me_m],
            send_sem=pm_send.at[k - 1], recv_sem=pm_recv.at[me_m],
            device_id={"member": lax.rem(me_m + k, members)}, device_id_type=MESH)

    def part_from_member(k):
        source = lax.rem(me_m + k, members)
        return pltpu.make_async_remote_copy(
            src_ref=part_src.at[0], dst_ref=parts_m.at[source],
            send_sem=pm_send.at[k - 1], recv_sem=pm_recv.at[source],
            device_id={"member": source}, device_id_type=MESH)

    def part_to_band(k):
        return pltpu.make_async_remote_copy(
            src_ref=part_src.at[1], dst_ref=parts_l.at[me_l],
            send_sem=pl_send.at[k - 1], recv_sem=pl_recv.at[me_l],
            device_id={"lat": lax.rem(me_l + k, bands)}, device_id_type=MESH)

    def part_from_band(k):
        source = lax.rem(me_l + k, bands)
        return pltpu.make_async_remote_copy(
            src_ref=part_src.at[1], dst_ref=parts_l.at[source],
            send_sem=pl_send.at[k - 1], recv_sem=pl_recv.at[source],
            device_id={"lat": source}, device_id_type=MESH)

    part_src[0] = partial

    for step in range(steps - 1, -1, -1):
        n = 2 * steps - 1 - step
        own = grads.at[step]
        for r in range(rows):
            if step == steps - 1:
                grads[step, r] = loss_grad[step, r]
            else:
                grads[step, r] = grads[step + 1, r] + change[r] + loss_grad[step, r]
        halo_start(n, own)
        if step == steps - 1:
            for k in range(1, members):
                part_to_member(k).start()
            parts_m[me_m] = partial
        else:
            if step == steps - 2:
                for k in range(1, members):
                    part_to_member(k).wait_send()
                    part_from_member(k).wait_recv()
                total = sum(parts_m[k] for k in range(members))
                part_src[1] = total
                for k in range(1, bands):
                    part_to_band(k).start()
                parts_l[me_l] = total
        widen_own(woutb, own)
        halo_wait(n, own)
        widen_rest(woutb, n)
        for j in range(rows + 2):
            put_hidden(j, before[:, j * cols:(j + 1) * cols] * slope[step, :, j * cols:(j + 1) * cols])
        change = narrow(winb)

    for r in range(rows):
        grad_ref[r] = grads[0, r] + change[r]
    for k in range(1, bands):
        part_to_band(k).wait_send()
        part_from_band(k).wait_recv()
    total = sum(parts_l[k] for k in range(bands))
    count = members * steps * rows * bands * chans * cols
    loss_ref[0, 0] = jnp.sum(total) / count


def on_device(members, bands, initial_states, targets, lat_weight, weight_in, weight_out, hidden_bias):
    steps, rows, chans, cols = targets.shape
    hidden = weight_in.shape[0]
    taps = 3 * chans
    depth = -(-taps // 256) * 256
    deep = 3 * hidden
    vmem = pl.BlockSpec(memory_space=pltpu.VMEM)
    smem = pl.BlockSpec(memory_space=pltpu.SMEM)
    dma = pltpu.SemaphoreType.DMA
    gradient, loss = pl.pallas_call(
        functools.partial(kernel, members, bands),
        out_shape=(jax.ShapeDtypeStruct((rows, chans, cols), F32), jax.ShapeDtypeStruct((1, 1), F32)),
        in_specs=[pl.BlockSpec(memory_space=pl.ANY)] * 6,
        out_specs=(vmem, smem),
        scratch_shapes=[
            pltpu.VMEM((rows, chans, cols), F32),
            pltpu.VMEM(targets.shape, F32),
            pltpu.VMEM((1, rows), F32),
            pltpu.VMEM((3 * taps, hidden), F32),
            pltpu.VMEM((chans, 3 * deep), F32),
            pltpu.VMEM((1, hidden), F32),
            dma((6,)),
            pltpu.VMEM((2 * steps, 2, 2, chans, cols), F32),
            pltpu.VMEM((steps, members - 1, rows, chans, cols), F32),
            pltpu.VMEM((members, 8, cols), F32),
            pltpu.VMEM((bands, 8, cols), F32),
            pltpu.VMEM((steps, rows, chans, cols), F32),
            pltpu.VMEM((steps, rows, chans, cols), F32),
            pltpu.VMEM((2, 8, cols), F32),
            pltpu.VMEM((3, 2 * hidden, depth), BF16),
            pltpu.VMEM((2 * taps, deep), BF16),
            pltpu.VMEM((2 * taps, deep), BF16),
            pltpu.VMEM((3, 2 * hidden, depth), BF16),
            pltpu.VMEM((depth, hidden), F32),
            pltpu.VMEM(((rows + 4) * depth, cols), BF16),
            pltpu.VMEM(((rows + 4) * depth, cols), BF16),
            pltpu.VMEM(((rows + 2) * hidden, cols), BF16),
            pltpu.VMEM(((rows + 2) * hidden, cols), BF16),
            pltpu.VMEM((hidden, (rows + 2) * cols), F32),
            pltpu.VMEM((steps, hidden, (rows + 2) * cols), F32),
            pltpu.VMEM((steps, rows, chans, cols), F32),
            pltpu.VMEM((hidden, cols), F32),
            dma((2 * steps, 2)), dma((2 * steps, 2)),
            dma((steps, members - 1)), dma((steps, members - 1)),
            dma((members - 1,)), dma((members,)),
            dma((bands - 1,)), dma((bands,)),
        ],
        compiler_params=pltpu.CompilerParams(collective_id=0, has_side_effects=True),
    )(
        initial_states.reshape(rows, chans, cols), targets, lat_weight.reshape(1, rows),
        weight_in.T, weight_out, hidden_bias.reshape(1, hidden),
    )
    return gradient.reshape(initial_states.shape), loss.reshape(())


def solution(mesh):
    placed = (P("member", "lat", None, None), P(None, "lat", None, None), P("lat"), P(), P(), P())
    return jax.shard_map(
        functools.partial(on_device, mesh.shape["member"], mesh.shape["lat"]),
        mesh=mesh,
        in_specs=placed,
        out_specs=(P("member", "lat", None, None), P()),
        check_vma=False,
    )
```

```python
import functools

import jax
import jax.numpy as jnp
from jax import lax
from jax.experimental import pallas as pl
from jax.experimental.pallas import tpu as pltpu
from jax.sharding import PartitionSpec as P

smooth_width = 0.1
gelu_scale = 0.7978845608028654
gelu_cubic = 0.044715
MESH = pl.DeviceIdType.MESH
F32 = jnp.float32
BF16 = jnp.bfloat16


def split(value):
    high = value.astype(BF16)
    low = (value - high.astype(F32)).astype(BF16)
    return high, low


def shifted(value, tap):
    if tap == 1:
        return value
    columns = value.shape[-1]
    lane = lax.broadcasted_iota(jnp.int32, value.shape, 1)
    if tap == 0:
        return jnp.where(lane == 0, 0.0, pltpu.roll(value, 1, 1))
    return jnp.where(lane == columns - 1, 0.0, pltpu.roll(value, columns - 1, 1))


def dot(left, right):
    return jnp.dot(left, right, preferred_element_type=F32)


def kernel(
    members, bands,
    x_hbm, target_hbm, lat_hbm, w_in_hbm, w_out_hbm, bias_hbm,
    grad_ref, loss_ref,
    x_ref, target_ref, lat_ref, w_in_ref, w_out_ref, bias_ref, fetch_sem,
    halo, others, parts_m, parts_l, fields, grads, part_src,
    win, winb, wout, woutb, tall, s_high, s_low, h_high, h_low, before, slope, loss_grad, bias,
    halo_send, halo_recv, other_send, other_recv, pm_send, pm_recv, pl_send, pl_recv,
):
    steps, rows, chans, cols = target_ref.shape
    hidden = w_in_ref.shape[1]
    taps = 3 * chans
    depth = win.shape[2]
    deep = 3 * hidden
    me_m = lax.axis_index("member")
    me_l = lax.axis_index("lat")
    has_up = me_l > 0
    has_down = me_l < bands - 1

    fetches = [
        pltpu.make_async_copy(source, target, fetch_sem.at[n])
        for n, (source, target) in enumerate([
            (x_hbm, x_ref), (w_in_hbm, w_in_ref), (w_out_hbm, w_out_ref),
            (bias_hbm, bias_ref), (target_hbm, target_ref), (lat_hbm, lat_ref)])
    ]
    barrier = pltpu.get_barrier_semaphore()
    for k in range(1, members):
        pl.semaphore_signal(barrier, inc=1, device_id={"member": lax.rem(me_m + k, members)}, device_id_type=MESH)
    for k in range(1, bands):
        pl.semaphore_signal(barrier, inc=1, device_id={"lat": lax.rem(me_l + k, bands)}, device_id_type=MESH)

    for fetch in fetches:
        fetch.start()

    @pl.when(jnp.logical_not(has_up))
    def _():
        for n in range(2 * steps):
            halo[n, 0] = jnp.zeros(halo.shape[2:], F32)

    @pl.when(jnp.logical_not(has_down))
    def _():
        for n in range(2 * steps):
            halo[n, 1] = jnp.zeros(halo.shape[2:], F32)

    def to_up(n, source):
        return pltpu.make_async_remote_copy(
            src_ref=source.at[0:2], dst_ref=halo.at[n, 1],
            send_sem=halo_send.at[n, 0], recv_sem=halo_recv.at[n, 1],
            device_id={"lat": jnp.maximum(me_l - 1, 0)}, device_id_type=MESH)

    def to_down(n, source):
        return pltpu.make_async_remote_copy(
            src_ref=source.at[rows - 2:rows], dst_ref=halo.at[n, 0],
            send_sem=halo_send.at[n, 1], recv_sem=halo_recv.at[n, 0],
            device_id={"lat": jnp.minimum(me_l + 1, bands - 1)}, device_id_type=MESH)

    def halo_start(n, source):
        @pl.when(has_up)
        def _():
            to_up(n, source).start()

        @pl.when(has_down)
        def _():
            to_down(n, source).start()

    def halo_wait(n, source):
        @pl.when(has_up)
        def _():
            to_up(n, source).wait_send()
            to_down(n, source).wait_recv()

        @pl.when(has_down)
        def _():
            to_down(n, source).wait_send()
            to_up(n, source).wait_recv()

    def to_member(step, k):
        return pltpu.make_async_remote_copy(
            src_ref=fields.at[step], dst_ref=others.at[step, k - 1],
            send_sem=other_send.at[step, k - 1], recv_sem=other_recv.at[step, k - 1],
            device_id={"member": lax.rem(me_m + k, members)}, device_id_type=MESH)

    fetches[0].wait()
    pl.semaphore_wait(barrier, members + bands - 2)
    halo_start(0, x_ref)

    def put_wide(target, a, block):
        tall[0:taps, :] = block
        high, low = split(tall[...].T)
        target[a, 0:hidden] = high
        target[a, hidden:2 * hidden] = low

    def front_weights():
        for fetch in fetches[1:]:
            fetch.wait()
        tall[taps:, :] = jnp.zeros((depth - taps, hidden), F32)
        for a in range(3):
            put_wide(win, a, w_in_ref[a * taps:(a + 1) * taps, :])
        bias[...] = jnp.broadcast_to(bias_ref[...], (cols, hidden)).T
        for j in range(rows + 4):
            s_high[j * depth + taps:(j + 1) * depth, :] = jnp.zeros((depth - taps, cols), BF16)
            s_low[j * depth + taps:(j + 1) * depth, :] = jnp.zeros((depth - taps, cols), BF16)

    def narrow_weights():
        for a in range(3):
            for b in range(3):
                at = (3 * a + b) * hidden
                high, low = split(w_out_ref[:, at:at + hidden])
                wout[b * chans:(b + 1) * chans, a * hidden:(a + 1) * hidden] = high
                wout[taps + b * chans:taps + (b + 1) * chans, a * hidden:(a + 1) * hidden] = low

    def back_weights():
        for a in range(3):
            for b in range(3):
                at = (3 * (2 - a) + 2 - b) * chans
                high, low = split(w_in_ref[at:at + chans, :])
                winb[b * chans:(b + 1) * chans, a * hidden:(a + 1) * hidden] = high
                winb[taps + b * chans:taps + (b + 1) * chans, a * hidden:(a + 1) * hidden] = low
        for a in range(3):
            at = 3 * (2 - a) * hidden
            put_wide(woutb, a, jnp.concatenate(
                [w_out_ref[:, at + (2 - b) * hidden:at + (3 - b) * hidden] for b in range(3)], axis=0))

    def put_line(i, line):
        for b in range(3):
            high, low = split(shifted(line, b))
            at = i * depth + b * chans
            s_high[at:at + chans, :] = high
            s_low[at:at + chans, :] = low

    def widen_part(weights, inside):
        sums = {}
        for a in range(3):
            lines = [j for j in range(rows + 2) if (2 <= j + a < rows + 2) == inside]
            high = jnp.concatenate([s_high[(j + a) * depth:(j + a + 1) * depth, :] for j in lines], axis=1)
            low = jnp.concatenate([s_low[(j + a) * depth:(j + a + 1) * depth, :] for j in lines], axis=1)
            both = dot(weights[a], high)
            total = both[0:hidden] + both[hidden:2 * hidden] + dot(weights[a, 0:hidden, :], low)
            for n, j in enumerate(lines):
                line = total[:, n * cols:(n + 1) * cols]
                sums[j] = line if j not in sums else sums[j] + line
        return sums

    def widen_own(weights, own):
        for r in range(rows):
            put_line(r + 2, own[r])
        for j, line in widen_part(weights, True).items():
            before[:, j * cols:(j + 1) * cols] = line

    def widen_rest(weights, n):
        for j in range(2):
            put_line(j, halo[n, 0, j])
            put_line(rows + 2 + j, halo[n, 1, j])
        for j, line in widen_part(weights, False).items():
            before[:, j * cols:(j + 1) * cols] += line

    def narrow(weights):
        right = jnp.concatenate([h_high[r * hidden:r * hidden + deep, :] for r in range(rows)], axis=1)
        both = dot(weights[...], right)
        right = jnp.concatenate([h_low[r * hidden:r * hidden + deep, :] for r in range(rows)], axis=1)
        total = both[0:taps] + both[taps:2 * taps] + dot(weights[0:taps, :], right)
        result = []
        for r in range(rows):
            line = total[:, r * cols:(r + 1) * cols]
            result.append(sum(shifted(line[b * chans:(b + 1) * chans], b) for b in range(3)))
        return result

    def put_hidden(j, value):
        if j == 0:
            value = jnp.where(has_up, value, 0.0)
        if j == rows + 1:
            value = jnp.where(has_down, value, 0.0)
        high, low = split(value)
        h_high[j * hidden:(j + 1) * hidden, :] = high
        h_low[j * hidden:(j + 1) * hidden, :] = low

    def fold(value):
        return sum(value[8 * i:8 * i + 8] for i in range(chans // 8))

    def loss_terms(step):
        partial = jnp.zeros((8, cols), F32)
        for r in range(rows):
            error = fields[step, r] - target_ref[step, r]
            square = error * error + smooth_width * smooth_width
            inverse = lax.rsqrt(square)
            scale = lat_ref[0:1, r:r + 1]
            partial = partial + scale * fold(square * inverse - smooth_width / (2.0 * (members - 1)))
            loss_grad[step, r] = scale * (error * inverse)
        for k in range(1, members):
            to_member(step, k).wait()
            for r in range(rows):
                spread = fields[step, r] - others[step, k - 1, r]
                square = spread * spread + smooth_width * smooth_width
                inverse = lax.rsqrt(square)
                scale = lat_ref[0:1, r:r + 1]
                partial = partial - scale / (2.0 * (members - 1)) * fold(square * inverse)
                loss_grad[step, r] = loss_grad[step, r] - scale / (members - 1) * (spread * inverse)
        return partial

    for step in range(steps):
        own = x_ref if step == 0 else fields.at[step - 1]
        if step == 0:
            front_weights()
        widen_own(win, own)
        if step == 0:
            narrow_weights()
        halo_wait(step, own)
        widen_rest(win, step)
        for j in range(rows + 2):
            value = before[:, j * cols:(j + 1) * cols] + bias[...]
            inner = jnp.tanh(gelu_scale * (value + gelu_cubic * value * value * value))
            put_hidden(j, 0.5 * value * (1.0 + inner))
            slope[step, :, j * cols:(j + 1) * cols] = 0.5 * (1.0 + inner) + 0.5 * value * (1.0 - inner * inner) * (
                gelu_scale * (1.0 + 3.0 * gelu_cubic * value * value))
        change = narrow(wout)
        for r in range(rows):
            fields[step, r] = own[r] + change[r]
        if step < steps - 1:
            halo_start(step + 1, fields.at[step])
        for k in range(1, members):
            to_member(step, k).start()
        if step == 0:
            back_weights()

    partial = jnp.zeros((8, cols), F32)
    for step in range(steps):
        partial = partial + loss_terms(step)

    def part_to_member(k):
        return pltpu.make_async_remote_copy(
            src_ref=part_src.at[0], dst_ref=parts_m.at[me_m],
            send_sem=pm_send.at[k - 1], recv_sem=pm_recv.at[me_m],
            device_id={"member": lax.rem(me_m + k, members)}, device_id_type=MESH)

    def part_from_member(k):
        source = lax.rem(me_m + k, members)
        return pltpu.make_async_remote_copy(
            src_ref=part_src.at[0], dst_ref=parts_m.at[source],
            send_sem=pm_send.at[k - 1], recv_sem=pm_recv.at[source],
            device_id={"member": source}, device_id_type=MESH)

    def part_to_band(k):
        return pltpu.make_async_remote_copy(
            src_ref=part_src.at[1], dst_ref=parts_l.at[me_l],
            send_sem=pl_send.at[k - 1], recv_sem=pl_recv.at[me_l],
            device_id={"lat": lax.rem(me_l + k, bands)}, device_id_type=MESH)

    def part_from_band(k):
        source = lax.rem(me_l + k, bands)
        return pltpu.make_async_remote_copy(
            src_ref=part_src.at[1], dst_ref=parts_l.at[source],
            send_sem=pl_send.at[k - 1], recv_sem=pl_recv.at[source],
            device_id={"lat": source}, device_id_type=MESH)

    part_src[0] = partial

    for step in range(steps - 1, -1, -1):
        n = 2 * steps - 1 - step
        own = grads.at[step]
        for r in range(rows):
            if step == steps - 1:
                grads[step, r] = loss_grad[step, r]
            else:
                grads[step, r] = grads[step + 1, r] + change[r] + loss_grad[step, r]
        halo_start(n, own)
        if step == steps - 1:
            for k in range(1, members):
                part_to_member(k).start()
            parts_m[me_m] = partial
        else:
            if step == steps - 2:
                for k in range(1, members):
                    part_to_member(k).wait_send()
                    part_from_member(k).wait_recv()
                total = sum(parts_m[k] for k in range(members))
                part_src[1] = total
                for k in range(1, bands):
                    part_to_band(k).start()
                parts_l[me_l] = total
        widen_own(woutb, own)
        halo_wait(n, own)
        widen_rest(woutb, n)
        for j in range(rows + 2):
            put_hidden(j, before[:, j * cols:(j + 1) * cols] * slope[step, :, j * cols:(j + 1) * cols])
        change = narrow(winb)

    for r in range(rows):
        grad_ref[r] = grads[0, r] + change[r]
    for k in range(1, bands):
        part_to_band(k).wait_send()
        part_from_band(k).wait_recv()
    total = sum(parts_l[k] for k in range(bands))
    count = members * steps * rows * bands * chans * cols
    loss_ref[0, 0] = jnp.sum(total) / count


def on_device(members, bands, initial_states, targets, lat_weight, weight_in, weight_out, hidden_bias):
    steps, rows, chans, cols = targets.shape
    hidden = weight_in.shape[0]
    taps = 3 * chans
    depth = -(-taps // 256) * 256
    deep = 3 * hidden
    vmem = pl.BlockSpec(memory_space=pltpu.VMEM)
    smem = pl.BlockSpec(memory_space=pltpu.SMEM)
    dma = pltpu.SemaphoreType.DMA
    gradient, loss = pl.pallas_call(
        functools.partial(kernel, members, bands),
        out_shape=(jax.ShapeDtypeStruct((rows, chans, cols), F32), jax.ShapeDtypeStruct((1, 1), F32)),
        in_specs=[pl.BlockSpec(memory_space=pl.ANY)] * 6,
        out_specs=(vmem, smem),
        scratch_shapes=[
            pltpu.VMEM((rows, chans, cols), F32),
            pltpu.VMEM(targets.shape, F32),
            pltpu.VMEM((1, rows), F32),
            pltpu.VMEM((3 * taps, hidden), F32),
            pltpu.VMEM((chans, 3 * deep), F32),
            pltpu.VMEM((1, hidden), F32),
            dma((6,)),
            pltpu.VMEM((2 * steps, 2, 2, chans, cols), F32),
            pltpu.VMEM((steps, members - 1, rows, chans, cols), F32),
            pltpu.VMEM((members, 8, cols), F32),
            pltpu.VMEM((bands, 8, cols), F32),
            pltpu.VMEM((steps, rows, chans, cols), F32),
            pltpu.VMEM((steps, rows, chans, cols), F32),
            pltpu.VMEM((2, 8, cols), F32),
            pltpu.VMEM((3, 2 * hidden, depth), BF16),
            pltpu.VMEM((2 * taps, deep), BF16),
            pltpu.VMEM((2 * taps, deep), BF16),
            pltpu.VMEM((3, 2 * hidden, depth), BF16),
            pltpu.VMEM((depth, hidden), F32),
            pltpu.VMEM(((rows + 4) * depth, cols), BF16),
            pltpu.VMEM(((rows + 4) * depth, cols), BF16),
            pltpu.VMEM(((rows + 2) * hidden, cols), BF16),
            pltpu.VMEM(((rows + 2) * hidden, cols), BF16),
            pltpu.VMEM((hidden, (rows + 2) * cols), F32),
            pltpu.VMEM((steps, hidden, (rows + 2) * cols), F32),
            pltpu.VMEM((steps, rows, chans, cols), F32),
            pltpu.VMEM((hidden, cols), F32),
            dma((2 * steps, 2)), dma((2 * steps, 2)),
            dma((steps, members - 1)), dma((steps, members - 1)),
            dma((members - 1,)), dma((members,)),
            dma((bands - 1,)), dma((bands,)),
        ],
        compiler_params=pltpu.CompilerParams(collective_id=0, has_side_effects=True),
    )(
        initial_states.reshape(rows, chans, cols), targets, lat_weight.reshape(1, rows),
        weight_in.T, weight_out, hidden_bias.reshape(1, hidden),
    )
    return gradient.reshape(initial_states.shape), loss.reshape(())


def solution(mesh):
    placed = (P("member", "lat", None, None), P(None, "lat", None, None), P("lat"), P(), P(), P())
    return jax.shard_map(
        functools.partial(on_device, mesh.shape["member"], mesh.shape["lat"]),
        mesh=mesh,
        in_specs=placed,
        out_specs=(P("member", "lat", None, None), P()),
        check_vma=False,
    )
```
